32 devices in a mesh: wide: 16 (over z, y, x), narrow: 2 (over core).
Axes of the slice: x: 2, y: 2, z: 4, core: 2. Of those that a mesh axis runs over, the one named last changes fastest.
Arguments:
- queries: bfloat16 [4096, 768], P(('wide', 'narrow')), may hold values from -40 to 40
- table: bfloat16 [2048, 768], P('wide'), may hold values from -6 to 6
- head: bfloat16 [768, 768], replicated, may hold values from -0.21875 to 0.21875
- pos_ids: int32 [4096], P(('wide', 'narrow')), may hold values from 0 to 2047, as said below
- neg_ids: int32 [4096, 8], P(('wide', 'narrow')), may hold values from 0 to 2047, as said below
- loss_weights: float32 [4096], P(('wide', 'narrow')), may hold values from 8 to 64
Outputs:
- d_queries: float32 [4096, 768], P(('wide', 'narrow'))
- d_table: float32 [2048, 768], P(('wide', 'narrow'))
- d_head: float32 [768, 768], replicated
The draws below stay inside these ranges and needn't reach their ends.
Inputs may be any that keep to these rules, and one draw needn't show every extreme that they name: `pos_ids`: the queries form aligned blocks of 128 (the queries of one device). Within a block at most 16 positives lie in one shard of 128 consecutive passage rows (shard = id // 128); one shard, the same for every block, holds exactly 16 of every block. `neg_ids`: within each aligned block of 128 queries, at most 96 of its 1024 negatives lie in one shard of 128 consecutive passage rows (shard = id // 128); one shard, the same for every block, holds exactly 96 of every block. Popular rows recur.
All inputs are finite; a program needn't handle non-finite values.
Results may differ from the reference program's by a relative error of at most 0.0063.
Values may be sent and summed in bfloat16 or wider, within the bound.
A program may use at most 64 MiB of HBM per device.

```python
import math
from functools import partial
import jax
import jax.numpy as jnp
from jax import lax

D = 768
NEG = 8
QRY_DEV = 128
ROWS_DEV = 128
POS_CAP = 16
NEG_CAP = 96
QUERIES = 4096
PASSAGES = 2048
N_WIDE = 16
N_NARROW = 2


def make_table(key):
    base = jax.random.fold_in(key, 11)
    values = jnp.clip(jax.random.normal(base, (PASSAGES, D), jnp.float32), -6.0, 6.0)
    return values


def spread_owners(block_key, count_slots, capacity, hottest):
    remain = count_slots - capacity
    lowest = max(1, -(-remain // (N_WIDE - 1)))
    len_key, order_key, mix_key = jax.random.split(block_key, 3)
    run_lengths = jax.random.randint(len_key, (N_WIDE - 1,), lowest, capacity + 1)
    others = jnp.arange(N_WIDE - 1, dtype=jnp.int32)
    others = others + (others >= hottest).astype(jnp.int32)
    others = jax.random.permutation(order_key, others)
    bounds = jnp.cumsum(run_lengths)
    positions = jnp.arange(remain, dtype=jnp.int32)
    bucket_of = jnp.sum((bounds[None, :] <= positions[:, None]).astype(jnp.int32), axis=1)
    owners = jnp.concatenate([jnp.full((capacity,), hottest, jnp.int32), others[bucket_of]])
    return jax.random.permutation(mix_key, owners)


def make_ids(key, per_query, capacity, salt):
    base = jax.random.fold_in(jax.random.fold_in(key, 23), salt)
    hot_key, pop_key, block_key, local_key = jax.random.split(base, 4)
    hottest = jax.random.randint(hot_key, (), 0, N_WIDE)
    blocks = N_WIDE * N_NARROW
    per_block = QRY_DEV * per_query
    spreader = partial(spread_owners, count_slots=per_block, capacity=capacity, hottest=hottest)
    owners = jax.vmap(spreader)(jax.random.split(block_key, blocks))
    picks = jax.random.randint(local_key, (blocks, per_block, 2), 0, ROWS_DEV)
    skewed = picks[:, :, 0] * picks[:, :, 1] // ROWS_DEV
    popular = jax.random.permutation(pop_key, jnp.arange(ROWS_DEV, dtype=jnp.int32))
    return (owners * ROWS_DEV + popular[skewed]).reshape(QUERIES, per_query)


def draw_pos_ids(key, part):
    return make_ids(key, 1, POS_CAP, 1).reshape(QUERIES)


def draw_neg_ids(key, part):
    return make_ids(key, NEG, NEG_CAP, 2)


def draw_table(key, part):
    return make_table(key).astype(jnp.bfloat16)


def draw_queries(key, part):
    table = make_table(key)
    positive = draw_pos_ids(key, part)
    negative = draw_neg_ids(key, part)
    noise = jax.random.normal(jax.random.fold_in(key, 31), (QUERIES, D), jnp.float32)
    noise = jnp.clip(noise, -6.0, 6.0)
    hard_sum = jnp.zeros((QUERIES, D), jnp.float32)
    for column in range(NEG):
        hard_sum = hard_sum + table[negative[:, column]]
    mixed = 0.8 * noise + 0.15 * table[positive] + 0.13 * hard_sum
    return mixed.astype(jnp.bfloat16)


def steps_of(rng, shape, pieces, least, largest):
    def one(dim, parts):
        steps = jax.random.uniform(jax.random.fold_in(jax.random.fold_in(rng, 6), dim), (parts,), jnp.float32, least / len(pieces), largest / len(pieces))
        return jnp.repeat(jnp.exp(steps), shape[dim] // parts).reshape((-1,) + (1,) * (len(shape) - dim - 1))

    loudness = one(*pieces[0])
    for cut in pieces[1:]:
        loudness = loudness * one(*cut)
    return loudness


def normal_values(stream_key, extent, width, most, kind=jnp.bfloat16):
    entries = jax.random.normal(stream_key, extent, jnp.float32) * width
    return jnp.minimum(jnp.maximum(entries, -most), most).astype(kind)


def setup_inputs(seed: int = 0) -> dict:
    splits = jax.random.split(jax.random.key(seed), 7)
    return {
        "queries": draw_queries(jax.random.fold_in(splits[6], 71), 0),
        "table": draw_table(jax.random.fold_in(splits[6], 71), 0),
        "head": normal_values(splits[2], (D, D), D ** -0.5, 0.21875),
        "pos_ids": draw_pos_ids(jax.random.fold_in(splits[6], 71), 0),
        "neg_ids": draw_neg_ids(jax.random.fold_in(splits[6], 71), 0),
        "loss_weights": jnp.clip(jnp.exp(math.log(64.0) - 2.0794415 * jax.random.uniform(splits[5], (QUERIES,), jnp.float32) ** steps_of(splits[5], (QUERIES,), ((0, 32),), -0.2, 0.2)), 8.0, 64.0),
    }


def reference(queries, table, head, pos_ids, neg_ids, loss_weights):
    scale = float(D) ** -0.5
    group = N_NARROW * QRY_DEV
    query_proj = jnp.dot(queries, head, preferred_element_type=jnp.float32).astype(jnp.bfloat16)
    table_proj = jnp.dot(table, head, preferred_element_type=jnp.float32).astype(jnp.bfloat16)
    positions = jnp.arange(group, dtype=jnp.int32)
    target = (positions[:, None] == positions[None, :]).astype(jnp.float32)

    def one_group(row_total, index):
        start = (index * group).astype(jnp.int32)
        query_block = lax.dynamic_slice_in_dim(query_proj, start, group, 0)
        pos_block = lax.dynamic_slice_in_dim(pos_ids, start, group, 0)
        neg_block = lax.dynamic_slice_in_dim(neg_ids, start, group, 0)
        weight_block = lax.dynamic_slice_in_dim(loss_weights, start, group, 0)
        keys = jnp.take(table_proj, pos_block, axis=0)
        negatives = jnp.take(table_proj, neg_block, axis=0)
        in_scores = jnp.dot(query_block, keys.T, preferred_element_type=jnp.float32) * scale
        neg_scores = jnp.einsum("bd,bnd->bn", query_block.astype(jnp.float32), negatives.astype(jnp.float32), precision=lax.Precision.HIGHEST) * scale
        top = jnp.maximum(jnp.max(in_scores, axis=1), jnp.max(neg_scores, axis=1))
        total = jnp.sum(jnp.exp(in_scores - top[:, None]), axis=1) + jnp.sum(jnp.exp(neg_scores - top[:, None]), axis=1)
        log_total = top + jnp.log(total)
        in_probs = jnp.exp(in_scores - log_total[:, None])
        neg_probs = jnp.exp(neg_scores - log_total[:, None])
        in_coef = (weight_block[:, None] * (in_probs - target) * scale).astype(jnp.bfloat16)
        neg_coef = (weight_block[:, None] * neg_probs * scale).astype(jnp.bfloat16)
        grad_query = jnp.dot(in_coef, keys, preferred_element_type=jnp.float32)
        grad_query = grad_query + jnp.einsum("bn,bnd->bd", neg_coef.astype(jnp.float32), negatives.astype(jnp.float32), precision=lax.Precision.HIGHEST)
        key_grad = jnp.dot(in_coef.T, query_block, preferred_element_type=jnp.float32)
        neg_grad = neg_coef.astype(jnp.float32)[:, :, None] * query_block.astype(jnp.float32)[:, None, :]
        row_total = row_total.at[pos_block].add(key_grad)
        row_total = row_total.at[neg_block.reshape(-1)].add(neg_grad.reshape(-1, D))
        return row_total, grad_query.astype(jnp.bfloat16)

    row_total, grad_blocks = lax.scan(one_group, jnp.zeros((PASSAGES, D), jnp.float32), jnp.arange(N_WIDE, dtype=jnp.int32))
    grad_query = grad_blocks.reshape(QUERIES, D)
    d_queries = jnp.dot(grad_query, head.T, preferred_element_type=jnp.float32)
    row_grad = row_total.astype(jnp.bfloat16)
    d_table = jnp.dot(row_grad, head.T, preferred_element_type=jnp.float32)
    d_head = jnp.dot(queries.T, grad_query, preferred_element_type=jnp.float32) + jnp.dot(table.T, row_grad, preferred_element_type=jnp.float32)
    return d_queries, d_table, d_head
```

```python
import jax
import jax.numpy as jnp
from jax import lax
from jax.sharding import PartitionSpec as P

BOTH = ("wide", "narrow")


def per_device(queries, table, head, pos_ids, neg_ids, loss_weights):
    wide_count = lax.axis_size("wide")
    narrow_count = lax.axis_size("narrow")
    width = queries.shape[1]
    shard_rows = table.shape[0]
    part_rows = shard_rows // narrow_count
    rows = shard_rows * wide_count
    scale = float(width) ** (-0.5)
    mine = lax.axis_index("narrow")
    my_table = lax.dynamic_slice_in_dim(table, mine * part_rows, part_rows, 0)
    my_proj = jnp.dot(my_table, head, preferred_element_type=jnp.float32).astype(jnp.bfloat16)
    table_proj = lax.all_gather(my_proj, BOTH, axis=0, tiled=True)
    group_pos = lax.all_gather(pos_ids, "narrow", axis=0, tiled=True)
    query_proj = jnp.dot(queries, head, preferred_element_type=jnp.float32).astype(jnp.bfloat16)
    columns = jnp.arange(rows, dtype=jnp.int32)
    key_count = jnp.sum((group_pos[:, None] == columns[None, :]).astype(jnp.float32), axis=0)
    own = (pos_ids[:, None] == columns[None, :]).astype(jnp.float32)
    count = jnp.broadcast_to(key_count[None, :], own.shape)
    for n in range(neg_ids.shape[1]):
        count = count + (neg_ids[:, n : n + 1] == columns[None, :]).astype(jnp.float32)
    scores = (
        lax.dot_general(
            query_proj, table_proj, (((1,), (1,)), ((), ())), preferred_element_type=jnp.float32
        )
        * scale
    )
    top = jnp.max(jnp.where(count > 0, scores, -jnp.inf), axis=1, keepdims=True)
    exps = jnp.where(count > 0, jnp.exp(jnp.minimum(scores - top, 0.0)), 0.0)
    total = jnp.sum(count * exps, axis=1, keepdims=True)
    probs = exps / total
    weight = loss_weights[:, None] * scale
    coef = (weight * probs).astype(jnp.bfloat16).astype(jnp.float32)
    own_coef = (weight * (probs - 1.0)).astype(jnp.bfloat16).astype(jnp.float32)
    coef = ((count - own) * coef + own * own_coef).astype(jnp.bfloat16)
    grad_query = jnp.dot(coef, table_proj, preferred_element_type=jnp.float32).astype(jnp.bfloat16)
    d_queries = lax.dot_general(
        grad_query, head, (((1,), (1,)), ((), ())), preferred_element_type=jnp.float32
    )
    row_partial = lax.dot_general(
        coef, query_proj, (((0,), (0,)), ((), ())), preferred_element_type=jnp.float32
    ).astype(jnp.bfloat16)
    pieces = lax.all_to_all(row_partial, BOTH, split_axis=0, concat_axis=0, tiled=True)
    row_grad = jnp.sum(pieces.reshape(-1, part_rows, width).astype(jnp.float32), axis=0)
    row_grad = row_grad.astype(jnp.bfloat16)
    d_table = lax.dot_general(
        row_grad, head, (((1,), (1,)), ((), ())), preferred_element_type=jnp.float32
    )
    head_part = lax.dot_general(
        queries, grad_query, (((0,), (0,)), ((), ())), preferred_element_type=jnp.float32
    )
    head_part = head_part + lax.dot_general(
        my_table, row_grad, (((0,), (0,)), ((), ())), preferred_element_type=jnp.float32
    )
    d_head = lax.psum(head_part, BOTH)
    return (d_queries, d_table, d_head)


def solution(mesh):
    placed = (
        P(BOTH, None),
        P("wide", None),
        P(),
        P(BOTH),
        P(BOTH, None),
        P(BOTH),
    )
    return jax.shard_map(
        per_device,
        mesh=mesh,
        in_specs=placed,
        out_specs=(P(BOTH, None), P(BOTH, None), P()),
        check_vma=False,
    )
```

```python
import functools

import jax
import jax.numpy as jnp
from jax import lax
from jax.experimental import pallas as pl
from jax.experimental.pallas import tpu as pltpu
from jax.sharding import PartitionSpec as P

BOTH = ("wide", "narrow")
MESH = pl.DeviceIdType.MESH
NT = (((1,), (1,)), ((), ()))
TN = (((0,), (0,)), ((), ()))
F32 = jnp.float32
BF16 = jnp.bfloat16


def dot(a, b, dims=(((1,), (0,)), ((), ()))):
    return lax.dot_general(a, b, dims, preferred_element_type=F32)


class Net:
    def __init__(self, wide, narrow, send_sem, recv_sem):
        self.wide, self.narrow, self.depth = wide, narrow, wide // 4
        self.send_sem, self.recv_sem = send_sem, recv_sem
        self.w = lax.axis_index("wide")
        self.n = lax.axis_index("narrow")
        self.z, self.y, self.x = self.w // 4, (self.w // 2) % 2, self.w % 2
        self.px = (self.w + 1 - 2 * self.x, self.n)
        self.py = (self.w + 2 - 4 * self.y, self.n)
        self.me = self.y * 2 + self.x
        self.xn = self.y * 2 + 1 - self.x
        self.yn = (1 - self.y) * 2 + self.x
        self.dg = (1 - self.y) * 2 + 1 - self.x
        self.base = self.n * 4
        self.used = 0
        self.started = []

    def zpeer(self, d):
        return (lax.rem(self.z + d, self.depth) * 4 + self.me, self.n)

    def zfrom(self, d):
        return lax.rem(self.z - d + self.depth, self.depth)

    def sibling(self, d):
        return (self.w, lax.rem(self.n + d, self.narrow))

    def sems(self, count):
        first = self.used
        self.used += count
        return first

    def send(self, src, dst, sem, device):
        copy = pltpu.make_async_remote_copy(
            src_ref=src,
            dst_ref=dst,
            send_sem=self.send_sem.at[sem],
            recv_sem=self.recv_sem.at[sem],
            device_id=device,
            device_id_type=MESH,
        )
        copy.start()
        self.started.append(copy)

    def arrive(self, dst, sem):
        pltpu.make_async_remote_copy(
            src_ref=dst,
            dst_ref=dst,
            send_sem=self.send_sem.at[sem],
            recv_sem=self.recv_sem.at[sem],
            device_id=self.px,
            device_id_type=MESH,
        ).wait_recv()

    def drain(self):
        for copy in self.started:
            copy.wait_send()
        self.started = []

    def barrier(self):
        sem = pltpu.get_barrier_semaphore()
        peers = [self.px, self.py]
        peers += [self.zpeer(d) for d in range(1, self.depth)]
        peers += [self.sibling(d) for d in range(1, self.narrow)]
        for peer in peers:
            pl.semaphore_signal(sem, inc=1, device_id=peer, device_id_type=MESH)
        pl.semaphore_wait(sem, len(peers))

    def gather(self, buf, during=None):
        depth, base, z = self.depth, self.base, self.z
        zs = self.sems(depth)
        xs, ys = self.sems(depth), self.sems(depth)
        ax, by = self.sems(depth), self.sems(depth)
        sib = self.sems(4 * self.narrow)

        def share(slot, block):
            for d in range(1, self.narrow):
                piece = buf.at[:, base + block]
                self.send(piece, piece, sib + slot * self.narrow + d, self.sibling(d))

        own = buf.at[:, base + self.me, z]
        for d in range(1, depth):
            self.send(own, own, zs + d, self.zpeer(d))
        self.send(own, own, xs, self.px)
        self.send(own, own, ys, self.py)
        if during is not None:
            during()
        for d in range(1, depth):
            piece = buf.at[:, base + self.me, self.zfrom(d)]
            self.arrive(piece, zs + d)
            self.send(piece, piece, xs + d, self.px)
            self.send(piece, piece, ys + d, self.py)
        share(0, self.me)
        for d in range(depth):
            k = self.zfrom(d) if d else z
            self.arrive(buf.at[:, base + self.yn, k], ys + d)
            piece = buf.at[0, base + self.yn, k]
            self.send(piece, piece, ax + d, self.px)
            self.arrive(buf.at[:, base + self.xn, k], xs + d)
            piece = buf.at[1, base + self.xn, k]
            self.send(piece, piece, by + d, self.py)
        share(1, self.yn)
        share(2, self.xn)
        for d in range(depth):
            k = self.zfrom(d) if d else z
            self.arrive(buf.at[0, base + self.dg, k], ax + d)
            self.arrive(buf.at[1, base + self.dg, k], by + d)
        share(3, self.dg)
        for d in range(1, self.narrow):
            theirs = lax.rem(self.n - d + self.narrow, self.narrow) * 4
            for slot, block in enumerate((self.me, self.yn, self.xn, self.dg)):
                self.arrive(buf.at[:, theirs + block], sib + slot * self.narrow + d)

    def start_scatter(self, out, r0):
        sib = self.sems(self.narrow)

        def give(d):
            theirs = lax.rem(self.n + d, self.narrow) * 4
            self.send(out.at[:, pl.ds(theirs, 4)], r0.at[d - 1], sib + d, self.sibling(d))

        return sib, give

    def scatter(self, sib, own, out, r0, r1, r2, stage, r3, during=None):
        base, depth = self.base, self.depth
        one, two, zs = self.sems(4), self.sems(2), self.sems(depth)
        for d in range(1, self.narrow):
            self.arrive(r0.at[d - 1], sib + d)

        def pair(h, block):
            total = own(h, block)
            for d in range(1, self.narrow):
                total = total + r0[d - 1, h, block].astype(F32)
            return total

        for slot, blocks in enumerate(((self.dg, self.dg), (self.xn, self.yn))):
            for h, peer in ((0, self.px), (1, self.py)):
                at = out.at[h, base + blocks[h]]
                at[...] = pair(h, blocks[h]).astype(BF16)
                self.send(at, r1.at[h, slot], one + 2 * slot + h, peer)
        for h, block, peer in ((0, self.yn, self.py), (1, self.xn, self.px)):
            self.arrive(r1.at[h, 0], one + h)
            at = out.at[h, base + block]
            total = pair(h, block) + r1[h, 0].astype(F32)
            if h == 0:
                stage[0] = total.astype(BF16)
                self.send(stage.at[0], r2.at[0], two, peer)
            else:
                stage[1] = total.astype(BF16)
                self.send(stage.at[1], r2.at[1], two + 1, peer)
        if during is not None:
            during()
        kept = []
        for h in range(2):
            self.arrive(r1.at[h, 1], one + 2 + h)
            self.arrive(r2.at[h], two + h)
            total = pair(h, self.me) + r1[h, 1].astype(F32) + r2[h].astype(F32)
            stage[2 + h] = total.astype(BF16)
        for d in range(1, depth):
            to = lax.rem(self.z + d, depth)
            self.send(stage.at[pl.ds(2, 2), to], r3.at[d - 1], zs + d, self.zpeer(d))
        z = self.z
        for h in range(2):
            total = own(h, self.me, z) + r1[h, 1, z].astype(F32) + r2[h, z].astype(F32)
            for d in range(1, self.narrow):
                total = total + r0[d - 1, h, self.me, z].astype(F32)
            kept.append(total)
        for d in range(1, depth):
            self.arrive(r3.at[d - 1], zs + d)
            for h in range(2):
                kept[h] = kept[h] + r3[d - 1, h].astype(F32)
        return kept


def kernel(
    wide, narrow, reduce_head,
    queries, table, head, ids, weights,
    d_queries, d_table, d_head,
    send_sem, recv_sem,
    tab, neg_count, key_count, scores, coef, qp_ref, gq_ref,
    own_grad, out_grad, r0, r1, r2, stage, r3,
    head_grad, *head_bufs,
):
    net = Net(wide, narrow, send_sem, recv_sem)
    width = queries.shape[1]
    half = width // 2
    part = tab.shape[3]
    batch = queries.shape[0]
    span = net.depth * part
    blocks = 4 * narrow
    negatives = ids.shape[1] - 1
    scale = float(width) ** (-0.5)
    halves = (slice(0, half), slice(half, width))
    base, me, z = net.base, net.me, net.z

    net.barrier()
    my_table = table[pl.ds(pl.multiple_of(net.n * part, part), part), :]
    my_proj = dot(my_table, head[...]).astype(BF16)
    for h in range(2):
        tab[h, base + me, z] = my_proj[:, halves[h]]

    def each_block(body, carry=None, count=blocks):
        if count <= 8:
            for b in range(count):
                carry = body(b, carry)
            return carry
        return lax.fori_loop(0, count, body, carry)

    def cols(b):
        return pl.ds(pl.multiple_of(b * span, span), span)

    def own_mask(b):
        column = b * span + lax.broadcasted_iota(jnp.int32, (batch, span), 1)
        return column, (ids[:, negatives : negatives + 1] == column).astype(F32)

    keys = net.sems(narrow)

    def prepare():
        def count(b, _):
            column, own = own_mask(b)
            key_count[0, :, cols(b)] = jnp.sum(own, axis=0, keepdims=True)
            total = jnp.zeros((batch, span), F32)
            for k in range(negatives):
                total = total + (ids[:, k : k + 1] == column).astype(F32)
            neg_count[:, cols(b)] = total
            return 0

        each_block(count, 0)
        for d in range(1, narrow):
            net.send(key_count.at[0], key_count.at[d], keys + d, net.sibling(d))
        qp_ref[...] = dot(queries[...], head[...]).astype(BF16)

    net.gather(tab, prepare)
    for d in range(1, narrow):
        net.arrive(key_count.at[d], keys + d)

    def tab_block(h, b):
        return tab[h, b].reshape(span, half)

    def score(b, top):
        total = key_count[0, :, cols(b)]
        for d in range(1, narrow):
            total = total + key_count[d, :, cols(b)]
        count = neg_count[:, cols(b)] + total
        neg_count[:, cols(b)] = count
        value = dot(qp_ref[:, halves[0]], tab_block(0, b), NT)
        value = (value + dot(qp_ref[:, halves[1]], tab_block(1, b), NT)) * scale
        value = jnp.where(count > 0, value, -jnp.inf)
        scores[:, cols(b)] = value
        return jnp.maximum(top, jnp.max(value, axis=1, keepdims=True))

    top = each_block(score, jnp.full((batch, 1), -jnp.inf, F32))

    def expo(b, total):
        value = jnp.exp(scores[:, cols(b)] - top)
        scores[:, cols(b)] = value
        return total + jnp.sum(neg_count[:, cols(b)] * value, axis=1, keepdims=True)

    total = each_block(expo, jnp.zeros((batch, 1), F32))
    inverse = 1.0 / total
    weight = weights[...] * scale

    def coefs(b, _):
        _, own = own_mask(b)
        prob = scores[:, cols(b)] * inverse
        plain = (weight * prob).astype(BF16).astype(F32)
        target = (weight * (prob - 1.0)).astype(BF16).astype(F32)
        value = (neg_count[:, cols(b)] - own) * plain + own * target
        coef[b] = value.astype(BF16)
        return 0

    each_block(coefs, 0)

    sib, give = net.start_scatter(out_grad, r0)
    for d in range(1, narrow):
        theirs = lax.rem(net.n + d, narrow) * 4
        for k in range(4):
            for h in range(2):
                grad = dot(coef[theirs + k], qp_ref[:, halves[h]], TN)
                out_grad[h, theirs + k] = grad.astype(BF16).reshape(net.depth, part, half)
        give(d)
    for k in range(4):
        for h in range(2):
            grad = dot(coef[base + k], qp_ref[:, halves[h]], TN)
            own_grad[h, k] = grad.reshape(net.depth, part, half)

    def query_side():
        for h in range(2):
            def add(b, acc):
                return acc + dot(coef[b], tab_block(h, b))

            acc = each_block(add, jnp.zeros((batch, half), F32))
            gq_ref[:, halves[h]] = acc.astype(BF16)
        d_queries[...] = dot(gq_ref[...], head[...], NT)
        for h in range(2):
            part_sum = dot(queries[...], gq_ref[:, halves[h]], TN)
            head_grad[h] = part_sum.reshape(head_grad.shape[1:])

    def rows_own(h, *at):
        return own_grad[(h,) + at]

    kept = net.scatter(sib, rows_own, out_grad, r0, r1, r2, stage, r3, query_side)
    row_grad = [k.astype(BF16) for k in kept]
    d_table[...] = dot(row_grad[0], head[:, halves[0]], NT) + dot(
        row_grad[1], head[:, halves[1]], NT
    )
    for h in range(2):
        part_sum = dot(my_table, row_grad[h], TN)
        head_grad[h] = head_grad[h] + part_sum.reshape(head_grad.shape[1:])
    if reduce_head:
        h_all, h_out, h0, h1, h2, h_stage, h3 = head_bufs
        sib, give = net.start_scatter(h_out, h0)
        for d in range(1, narrow):
            theirs = lax.rem(net.n + d, narrow) * 4
            for h in range(2):
                h_out[h, pl.ds(theirs, 4)] = head_grad[h, pl.ds(theirs, 4)].astype(BF16)
            give(d)

        def head_own(h, block, *at):
            return head_grad[(h, base + block) + at]

        kept = net.scatter(sib, head_own, h_out, h0, h1, h2, h_stage, h3)
        for h in range(2):
            h_all[h, base + me, z] = kept[h].astype(BF16)
        net.gather(h_all)
        for h in range(2):
            d_head[:, halves[h]] = h_all[h].astype(F32).reshape(width, half)
    else:
        for h in range(2):
            d_head[:, halves[h]] = head_grad[h].reshape(width, half)
    net.drain()


def per_device(queries, table, head, pos_ids, neg_ids, loss_weights):
    wide = lax.axis_size("wide")
    narrow = lax.axis_size("narrow")
    batch, width = queries.shape
    half = width // 2
    shard = table.shape[0]
    part = shard // narrow
    depth = wide // 4
    rows = shard * wide
    span = depth * part
    blocks = 4 * narrow
    reduce_head = width % (8 * wide * narrow) == 0
    ids = jnp.concatenate([neg_ids, pos_ids[:, None]], axis=1)
    owner, local = ids // shard, ids % shard
    ids = (local // part) * (wide * part) + (owner % 4) * span + (owner // 4) * part + local % part

    def scatter_bufs(height):
        return [
            pltpu.VMEM((2, blocks, depth, height, half), BF16),
            pltpu.VMEM((narrow - 1, 2, 4, depth, height, half), BF16),
            pltpu.VMEM((2, 2, depth, height, half), BF16),
            pltpu.VMEM((2, depth, height, half), BF16),
            pltpu.VMEM((4, depth, height, half), BF16),
            pltpu.VMEM((depth - 1, 2, height, half), BF16),
        ]

    scratch = [
        pltpu.VMEM((2, blocks, depth, part, half), BF16),
        pltpu.VMEM((batch, rows), F32),
        pltpu.VMEM((narrow, 1, rows), F32),
        pltpu.VMEM((batch, rows), F32),
        pltpu.VMEM((blocks, batch, span), BF16),
        pltpu.VMEM((batch, width), BF16),
        pltpu.VMEM((batch, width), BF16),
        pltpu.VMEM((2, 4, depth, part, half), F32),
    ] + scatter_bufs(part)
    if reduce_head:
        height = width // (wide * narrow)
        scratch.append(pltpu.VMEM((2, blocks, depth, height, half), F32))
        scratch.append(pltpu.VMEM((2, blocks, depth, height, half), BF16))
        scratch += scatter_bufs(height)
    else:
        scratch.append(pltpu.VMEM((2, width, half), F32))
    count = 2 * (6 * depth + 6 + 5 * narrow) + narrow
    sems = [pltpu.SemaphoreType.DMA((count,)), pltpu.SemaphoreType.DMA((count,))]
    vmem = pl.BlockSpec(memory_space=pltpu.VMEM)
    d_queries, d_table, d_head = pl.pallas_call(
        functools.partial(kernel, wide, narrow, reduce_head),
        out_shape=(
            jax.ShapeDtypeStruct((batch, width), F32),
            jax.ShapeDtypeStruct((part, width), F32),
            jax.ShapeDtypeStruct((width, width), F32),
        ),
        in_specs=[vmem] * 5,
        out_specs=(vmem,) * 3,
        scratch_shapes=sems + scratch,
        compiler_params=pltpu.CompilerParams(
            collective_id=0, has_side_effects=True, vmem_limit_bytes=60 * 1024 * 1024
        ),
    )(queries, table, head, ids, loss_weights[:, None])
    if not reduce_head:
        d_head = lax.psum(d_head, BOTH)
    return (d_queries, d_table, d_head)


def solution(mesh):
    placed = (
        P(BOTH, None),
        P("wide", None),
        P(),
        P(BOTH),
        P(BOTH, None),
        P(BOTH),
    )
    return jax.shard_map(
        per_device,
        mesh=mesh,
        in_specs=placed,
        out_specs=(P(BOTH, None), P(BOTH, None), P()),
        check_vma=False,
    )
```
